32 devices in a mesh: obs: 4 (over z), td: 8 (over y, x, core).
Axes of the slice: x: 2, y: 2, z: 4, core: 2. Of those that a mesh axis runs over, the one named last changes fastest.
Arguments:
- timestreams: bfloat16 [4, 128, 8192], P('obs', 'td'), may hold values from -6 to 6
- filter_taps: bfloat16 [4, 128, 8, 129], P('obs', 'td'), may hold values from -0.5 to 0.5
- scan_bounds: int32 [4, 32], P('obs'), may hold values from 0 to 8192, as said below
- tile_index: int32 [4, 64], P('obs', 'td'), may hold values from 0 to 15
- det_weights: bfloat16 [4, 128], P('obs'), may hold values from 0.29882812 to 3
- positions: float32 [2, 128], replicated, may hold values from -1 to 1
- wafer_group: int32 [128], replicated, may hold values from 0 to 7, as said below
Outputs:
- filtered_residual: float32 [4, 128, 8192], P('obs', 'td')
- sky_map: float32 [16, 128, 128], P(None, ('obs', 'td'))
The draws below stay inside these ranges and needn't reach their ends.
Inputs may be any that keep to these rules, and one draw needn't show every extreme that they name: `scan_bounds`: each row is strictly increasing, starts with 0 and ends with 8192. `wafer_group`: every wafer group holds the same number of detectors.
All inputs are finite; a program needn't handle non-finite values.
Results may differ from the reference program's by a relative error of at most 0.009.
Values may be sent and summed in bfloat16 or wider, within the bound.
A program may use at most 128 MiB of HBM per device.

```python
import math
import jax
import jax.numpy as jnp
from jax import lax

TAPS = 129
BANDS = 8
TILE = 128
WAFERS = 8
POLY = 6
NINT = 16
OBS = 4
DET = 128
SAMP = 8192
TILES = 16


def draw_wafer_group(key, part):
    order = jax.random.permutation(jax.random.fold_in(key, 17), DET)
    return (order % WAFERS).astype(jnp.int32)


def draw_scan_bounds(key, part):
    keys = jax.random.split(jax.random.fold_in(key, 29), OBS)

    def one_row(row_key):
        inner = jax.random.permutation(row_key, SAMP - 1)[:2 * NINT - 2] + 1
        inner = jnp.sort(inner.astype(jnp.int32))
        return jnp.concatenate([jnp.zeros((1,), jnp.int32), inner, jnp.full((1,), SAMP, jnp.int32)])
    return jax.vmap(one_row)(keys)


def touch_ends(array, rng, low, high):
    shape = array.shape
    place = [jax.random.randint(jax.random.fold_in(rng, axis), (), 0, shape[axis]) for axis in range(len(shape))]
    array = array.at[tuple(place)].set(low)
    longest = shape.index(max(shape))
    place[longest] = (place[longest] + 1) % shape[longest]
    return array.at[tuple(place)].set(high)


def block_scale(stream_key, extent, cuts, smallest, largest):
    factor_of = 1.0
    for position, blocks in cuts:
        steps = jax.random.uniform(jax.random.fold_in(jax.random.fold_in(stream_key, 6), position), (blocks,), jnp.float32, smallest / len(cuts), largest / len(cuts))
        factor_of = factor_of * jnp.repeat(jnp.exp(steps), extent[position] // blocks).reshape((-1,) + (1,) * (len(extent) - 1 - position))
    return factor_of


def noise(rng, extent, width, limit, shards=(), held_as=jnp.bfloat16):
    entries = width * jax.random.normal(rng, extent, jnp.float32)
    if shards:
        entries = entries * block_scale(rng, extent, shards, -0.22, 0.18)
    return jnp.clip(entries, -limit, limit).astype(held_as)


def setup_inputs(seed: int = 0) -> dict:
    streams_of = jax.random.split(jax.random.key(seed), 8)
    return {
        "timestreams": noise(streams_of[0], (OBS, DET, SAMP), 1.0, 6.0, ((0, 4), (1, 8))),
        "filter_taps": noise(streams_of[1], (OBS, DET, BANDS, TAPS), TAPS ** -0.5, 0.5, ((0, 4), (1, 8))),
        "scan_bounds": draw_scan_bounds(jax.random.fold_in(streams_of[7], 71), 0),
        "tile_index": touch_ends(jax.random.randint(streams_of[3], (OBS, SAMP // TILE), 0, TILES), jax.random.fold_in(streams_of[3], 1), 0, TILES - 1).astype(jnp.int32),
        "det_weights": jnp.clip(jnp.exp(math.log(3.0) - 2.306499 * jax.random.uniform(streams_of[4], (OBS, DET), jnp.float32) ** block_scale(streams_of[4], (OBS, DET), ((0, 4),), -0.2, 0.2)), 0.29882812, 3.0).astype(jnp.bfloat16),
        "positions": jnp.clip(jax.random.uniform(streams_of[5], (2, DET), jnp.float32, -1.0, 1.0), -1.0, 1.0),
        "wafer_group": draw_wafer_group(jax.random.fold_in(streams_of[7], 71), 0),
    }


prior_weight = 1.0

def toeplitz(band_taps):
    leading = band_taps.shape[:-1]
    half = TAPS // 2
    padded = jnp.concatenate([jnp.zeros(leading + (TILE - half,), band_taps.dtype), band_taps, jnp.zeros(leading + (3 * TILE - TAPS + half,), band_taps.dtype)], axis=-1)
    repeated = jnp.tile(padded, (1,) * len(leading) + (TILE,))
    repeated = repeated[..., :TILE * (4 * TILE - 1)].reshape(leading + (TILE, 4 * TILE - 1))
    return repeated[..., :3 * TILE]

def windows_of(signal):
    blocks = jnp.pad(signal, ((0, 0), (0, 0), (TILE, TILE)))
    blocks = blocks.reshape(signal.shape[0], signal.shape[1], -1, TILE)
    return jnp.concatenate([blocks[:, :, :-2], blocks[:, :, 1:-1], blocks[:, :, 2:]], axis=-1)

def forward_filter(signal, filter_taps):
    windows = windows_of(signal)
    per_band = windows.shape[2] // BANDS
    pieces = []
    for band_idx in range(BANDS):
        kernel = toeplitz(filter_taps[:, :, band_idx]).astype(jnp.float32)
        band_part = windows[:, :, band_idx * per_band:(band_idx + 1) * per_band].astype(jnp.float32)
        pieces.append(jnp.einsum('odnj,odij->odni', band_part, kernel, precision=lax.Precision.HIGHEST))
    return jnp.concatenate(pieces, axis=2).reshape(signal.shape)

def adjoint_filter(signal, filter_taps):
    blocks = signal.reshape(signal.shape[0], signal.shape[1], -1, TILE)
    per_band = blocks.shape[2] // BANDS
    pieces = []
    for band_idx in range(BANDS):
        kernel = toeplitz(filter_taps[:, :, band_idx]).astype(jnp.float32)
        band_part = blocks[:, :, band_idx * per_band:(band_idx + 1) * per_band].astype(jnp.float32)
        pieces.append(jnp.einsum('odni,odij->odnj', band_part, kernel, precision=lax.Precision.HIGHEST))
    spread = jnp.concatenate(pieces, axis=2)
    zero_block = jnp.zeros(spread.shape[:2] + (1, TILE), jnp.float32)
    from_next = jnp.concatenate([spread[:, :, 1:, :TILE], zero_block], axis=2)
    from_prev = jnp.concatenate([zero_block, spread[:, :, :-1, 2 * TILE:]], axis=2)
    summed = spread[:, :, :, TILE:2 * TILE] + from_next + from_prev
    return summed.reshape(signal.shape)

def make_basis(positions, wafer_group):
    x_pos = positions[0]
    y_pos = positions[1]
    monomials = jnp.stack([jnp.ones_like(x_pos), x_pos, y_pos, x_pos * x_pos, x_pos * y_pos, y_pos * y_pos])
    member = (wafer_group[None, :] == jnp.arange(WAFERS, dtype=jnp.int32)[:, None]).astype(jnp.float32)
    basis_b = (member[:, None, :] * monomials[None]).reshape(WAFERS * POLY, -1).astype(jnp.bfloat16)
    basis_f = basis_b.astype(jnp.float32)
    gram_matrix = jnp.dot(basis_f, basis_f.T, precision=lax.Precision.HIGHEST)
    factor = jnp.linalg.cholesky(gram_matrix)
    lower_inv = lax.linalg.triangular_solve(factor, jnp.eye(WAFERS * POLY, dtype=jnp.float32), left_side=True, lower=True)
    inverse = jnp.dot(lower_inv.T, lower_inv, precision=lax.Precision.HIGHEST)
    return (basis_b, basis_f, inverse)

def remove_poly(gathered, basis):
    basis_b, basis_f, inverse = basis
    coef_raw = jnp.einsum('md,nds->nms', basis_f, gathered.astype(jnp.float32), precision=lax.Precision.HIGHEST)
    coefficients = jnp.einsum('mq,nqs->nms', inverse, coef_raw, precision=lax.Precision.HIGHEST)
    fitted = jnp.einsum('md,nms->nds', basis_f, coefficients, precision=lax.Precision.HIGHEST)
    return (gathered.astype(jnp.float32) - fitted).astype(jnp.bfloat16)

def scan_flags(bounds, offset, length):
    sample = offset + jnp.arange(length, dtype=jnp.int32)
    passed = jnp.sum((bounds[:, :, None] <= sample[None, None, :]).astype(jnp.int32), axis=1)
    return (passed % 2).astype(jnp.float32)

def bin_maps(cleaned, in_scan, det_weights, tile_index):
    obs_count, det_count, samples = cleaned.shape
    groups = det_count // TILE
    block_count = samples // TILE
    masked = cleaned.astype(jnp.float32) * in_scan[:, None, :]
    shaped = masked.reshape(obs_count, groups, TILE, block_count, TILE)
    weight_rows = det_weights.astype(jnp.float32).reshape(obs_count, groups, TILE)
    block_sums = jnp.einsum('oqr,oqrbc->obrc', weight_rows, shaped, precision=lax.Precision.HIGHEST)
    row_weight = jnp.sum(weight_rows, axis=1)
    one_hot = (tile_index[:, :, None] == jnp.arange(TILES, dtype=jnp.int32)[None, None, :]).astype(jnp.float32)
    weighted_sum = jnp.einsum('obt,obrc->trc', one_hot, block_sums, precision=lax.Precision.HIGHEST)
    scan_blocks = in_scan.reshape(obs_count, block_count, TILE)
    hit_weight = jnp.einsum('obt,or,obc->trc', one_hot, row_weight, scan_blocks, precision=lax.Precision.HIGHEST)
    return (weighted_sum, hit_weight, one_hot)

def rescan_residual(cleaned, in_scan, sky_b, one_hot):
    obs_count, det_count, samples = cleaned.shape
    groups = det_count // TILE
    block_count = samples // TILE
    selected = jnp.einsum('obt,trc->orbc', one_hot, sky_b.astype(jnp.float32), precision=lax.Precision.HIGHEST)
    shaped = cleaned.astype(jnp.float32).reshape(obs_count, groups, TILE, block_count, TILE)
    deviation = shaped - selected[:, None]
    flags = in_scan.reshape(obs_count, 1, 1, block_count, TILE)
    return (flags * deviation).astype(jnp.bfloat16).reshape(obs_count, det_count, samples)

def reference(timestreams, filter_taps, scan_bounds, tile_index, det_weights, positions, wafer_group):
    basis = make_basis(positions, wafer_group)
    weighted_sum = jnp.zeros((TILES, TILE, TILE), jnp.float32)
    hit_weight = jnp.zeros((TILES, TILE, TILE), jnp.float32)
    kept = []
    for obs_idx in range(OBS):
        filtered = forward_filter(timestreams[obs_idx:obs_idx + 1], filter_taps[obs_idx:obs_idx + 1]).astype(jnp.bfloat16)
        cleaned = remove_poly(filtered, basis)
        in_scan = scan_flags(scan_bounds[obs_idx:obs_idx + 1], 0, SAMP)
        part_sum, part_hit, one_hot = bin_maps(cleaned, in_scan, det_weights[obs_idx:obs_idx + 1], tile_index[obs_idx:obs_idx + 1])
        weighted_sum = weighted_sum + part_sum
        hit_weight = hit_weight + part_hit
        kept.append((cleaned, in_scan, one_hot))
    sky_map = weighted_sum / (hit_weight + prior_weight)
    sky_b = sky_map.astype(jnp.bfloat16)
    outputs = []
    for obs_idx in range(OBS):
        cleaned, in_scan, one_hot = kept[obs_idx]
        residual = rescan_residual(cleaned, in_scan, sky_b, one_hot)
        outputs.append(adjoint_filter(residual, filter_taps[obs_idx:obs_idx + 1]))
    return (jnp.concatenate(outputs, axis=0), sky_map)
```

```python
import functools

import jax
import jax.numpy as jnp
from jax import lax
from jax.experimental import pallas as pl
from jax.experimental.pallas import tpu as pltpu
from jax.sharding import PartitionSpec as P

TAPS = 129
HALF = 64
BANDS = 8
TILE = 128
POLY = 6
TILES = 16
LANES = 128
prior_weight = 1.0
F32 = jnp.float32
BF16 = jnp.bfloat16


def lane_band(det):
    return lax.broadcasted_iota(jnp.int32, (HALF, LANES), 1) // det


def projector(pos_ref, wafer_ref, dets):
    x = pos_ref[0:1, :]
    y = pos_ref[1:2, :]
    rows = [jnp.ones_like(x), x, y, x * x, x * y, y * y]
    q = [r.astype(BF16).astype(F32) for r in rows]
    group = jnp.broadcast_to(wafer_ref[...].astype(F32), (dets, dets))
    same = group == group.T
    same_b = jnp.where(same, 1.0, 0.0).astype(BF16)
    pairs = [(i, j) for i in range(POLY) for j in range(i + 1)]
    products = jnp.concatenate(
        [q[i] * q[j] for i, j in pairs] + [jnp.zeros((32 - len(pairs), dets), F32)], axis=0
    )
    high = products.astype(BF16)
    low = (products - high.astype(F32)).astype(BF16)
    gram = jnp.dot(high, same_b, preferred_element_type=F32) + jnp.dot(
        low, same_b, preferred_element_type=F32
    )
    entry = {pair: gram[n : n + 1, :] for n, pair in enumerate(pairs)}
    factor, inv, white = {}, {}, []
    for i in range(POLY):
        for j in range(i + 1):
            value = entry[(i, j)]
            for k in range(j):
                value = value - factor[(i, k)] * factor[(j, k)]
            if i == j:
                factor[(i, i)] = jnp.sqrt(value)
                inv[i] = 1.0 / factor[(i, i)]
            else:
                factor[(i, j)] = value * inv[j]
        value = q[i]
        for k in range(i):
            value = value - factor[(i, k)] * white[k]
        white.append(value * inv[i])
    whitened = jnp.concatenate(white + [jnp.zeros((8 - POLY, dets), F32)], axis=0)
    columns = jnp.concatenate([whitened, jnp.zeros((LANES - 8, dets), F32)], axis=0).T
    outer = columns[:, 0:1] * white[0]
    for m in range(1, POLY):
        outer = outer + columns[:, m : m + 1] * white[m]
    outer = jnp.where(same, outer, 0.0)
    p_high = outer.astype(BF16)
    p_low = (outer - p_high.astype(F32)).astype(BF16)
    return p_high, p_low


def clean(p_high, p_low, gathered):
    fitted = jnp.dot(p_high, gathered, preferred_element_type=F32) + jnp.dot(
        p_low, gathered, preferred_element_type=F32
    )
    return (gathered.astype(F32) - fitted).astype(BF16)


def scan_mask(bounds_ref, rows, n_bounds):
    sample = lax.broadcasted_iota(jnp.int32, (rows, TILE), 0) * TILE + lax.broadcasted_iota(
        jnp.int32, (rows, TILE), 1
    )
    count = jnp.zeros((rows, TILE), jnp.int32)
    for n in range(n_bounds):
        count = count + jnp.where(bounds_ref[0, n] <= sample, 1, 0)
    return (count & 1).astype(F32)


def own_weights(weights_ref, start, det, dets):
    pick = lax.broadcasted_iota(jnp.int32, (dets, LANES), 0) == start + lax.broadcasted_iota(
        jnp.int32, (dets, LANES), 1
    ) % det
    rows = jnp.broadcast_to(weights_ref[...].astype(F32), (16, dets)).astype(BF16)
    return jnp.dot(rows, jnp.where(pick, 1.0, 0.0).astype(BF16), preferred_element_type=F32)[0:1, :]


def load_taps(raw_ref, low_ref, last_ref, taps_ref, det):
    for d in range(det):
        value = raw_ref[d].astype(F32)
        low_ref[d * BANDS : (d + 1) * BANDS, :] = value[:, 0:LANES]
        last_ref[d * BANDS : (d + 1) * BANDS, :] = jnp.broadcast_to(
            value[:, LANES:TAPS], (BANDS, LANES)
        )
    low = [low_ref[pl.ds(b, det, stride=BANDS), :] for b in range(BANDS)]
    last = [last_ref[pl.ds(b, det, stride=BANDS), :] for b in range(BANDS)]
    taps_ref[0:LANES, :] = jnp.concatenate(low, axis=0).T
    taps_ref[LANES:TAPS, :] = jnp.concatenate(last, axis=0).T[0:1, :]


def build_toeplitz(low_ref, last_ref, toep_ref, det):
    lead = lax.broadcasted_iota(jnp.int32, (TILE, LANES), 1) - lax.broadcasted_iota(
        jnp.int32, (TILE, LANES), 0
    )
    inner = (lead >= -HALF) & (lead < HALF)

    def one(d, _):
        for b in range(BANDS):
            n = d * BANDS + b
            row = jnp.broadcast_to(low_ref[pl.ds(n, 1), :], (TILE, LANES))
            last = jnp.broadcast_to(last_ref[pl.ds(n, 1), :], (TILE, LANES))
            ring = pltpu.roll(row, HALF, 1, stride=1, stride_axis=0)
            here = jnp.where(inner, ring, jnp.where(lead == HALF, last, 0.0))
            away = jnp.where(inner, jnp.where(lead == -HALF, last, 0.0), ring)
            toep_ref[n, :, 0:LANES] = here.astype(BF16)
            toep_ref[n, :, LANES : 2 * LANES] = away.astype(BF16)
        return 0

    lax.fori_loop(0, det, one, 0)


MESH = pl.DeviceIdType.MESH
PIECES = 4


def load_signal(x_ref, ext_ref, length, det):
    for c in range(length // TILE):
        piece = jnp.concatenate(
            [x_ref[:, b * length + c * TILE : b * length + (c + 1) * TILE] for b in range(BANDS)],
            axis=0,
        )
        ext_ref[HALF + c * TILE : HALF + (c + 1) * TILE, :] = piece.astype(F32).T
    band = lane_band(det)
    last = ext_ref[length : length + HALF, :]
    first = ext_ref[HALF : 2 * HALF, :]
    ext_ref[0:HALF, :] = jnp.where(band > 0, pltpu.roll(last, det, 1), 0.0)
    ext_ref[HALF + length : 2 * HALF + length, :] = jnp.where(
        band < BANDS - 1, pltpu.roll(first, LANES - det, 1), 0.0
    )


def whole_kernel(
    dims, bounds_ref, index_ref, x_hbm, taps_hbm, weights_ref, pos_ref, wafer_ref,
    out_ref, skyout_ref,
    x_ref, raw_ref, low_ref, last_ref, taps_ref, toep_ref, clean_ref, edge_ref, wide_ref,
    ext_ref, mask_ref, fsend, frecv, csend, crecv, tsend, trecv,
    msend, mrecv, nsend, nrecv, sky_ref, skyrecv,
    f_s, f_r, c_s, c_r, t_s, t_r, m_s, m_r, n_s, n_r, k_s, k_r, in_s,
):
    n_obs, td, det, length, slab, n_bounds = dims
    dets = det * td
    split = td // BANDS
    blocks = slab // TILE
    width = slab // PIECES
    folds = dets // TILE
    per_fold = td // folds
    parts = n_obs * folds
    own_rows = TILE // (n_obs * td)
    obs = lax.axis_index("obs")
    me = lax.axis_index("td")
    member = obs * folds + me // per_fold

    def td_peer(k):
        return lax.rem(me + k, td)

    def td_source(k):
        return lax.rem(me + td - k, td)

    def part_peer(k):
        m = lax.rem(member + k, parts)
        return (m // folds, lax.rem(me, per_fold) + lax.rem(m, folds) * per_fold)

    def part_source(k):
        return lax.rem(member + parts - k, parts)

    fold = me // per_fold
    first_row = own_rows * (obs * td + fold * per_fold)
    row_source = fold * per_fold + (own_rows * (obs * td + me)) // det
    x_copy = pltpu.make_async_copy(x_hbm, x_ref, in_s.at[0])
    raw_copy = pltpu.make_async_copy(taps_hbm, raw_ref, in_s.at[1])
    x_copy.start()
    raw_copy.start()

    barrier = pltpu.get_barrier_semaphore()
    for k in range(1, td):
        pl.semaphore_signal(barrier, 1, device_id=(obs, td_peer(k)), device_id_type=MESH)
    for k in range(1, parts):
        pl.semaphore_signal(barrier, 1, device_id=part_peer(k), device_id_type=MESH)

    row = lax.broadcasted_iota(jnp.int32, (blocks, LANES), 0)
    tile = jnp.zeros((blocks, LANES), jnp.int32)
    for n in range(blocks):
        tile = jnp.where(row == n, index_ref[0, n], tile)
    tsend[...] = tile.astype(F32)
    trecv[me] = tile.astype(F32)
    raw_copy.wait()
    load_taps(raw_ref, low_ref, last_ref, taps_ref, det)
    x_copy.wait()
    load_signal(x_ref, ext_ref, length, det)

    def tile_copy(k, slot):
        return pltpu.make_async_remote_copy(
            src_ref=tsend, dst_ref=trecv.at[slot], send_sem=t_s.at[k], recv_sem=t_r.at[k],
            device_id=(obs, td_peer(k)), device_id_type=MESH,
        )

    def signal_copy(h, k, slot):
        cols = pl.ds(pl.multiple_of(h * width, TILE), width)
        peer = td_peer(k)
        return pltpu.make_async_remote_copy(
            src_ref=fsend.at[peer, :, cols], dst_ref=frecv.at[slot, :, cols],
            send_sem=f_s.at[h, k], recv_sem=f_r.at[h, k],
            device_id=(obs, peer), device_id_type=MESH,
        )

    def clean_copy(h, k, slot):
        cols = pl.ds(pl.multiple_of(h * width, TILE), width)
        peer = td_peer(k)
        return pltpu.make_async_remote_copy(
            src_ref=csend.at[peer, :, cols], dst_ref=crecv.at[slot, :, cols],
            send_sem=c_s.at[h, k], recv_sem=c_r.at[h, k],
            device_id=(obs, peer), device_id_type=MESH,
        )

    def hit_copy(k, slot):
        return pltpu.make_async_remote_copy(
            src_ref=msend, dst_ref=mrecv.at[slot], send_sem=m_s.at[k], recv_sem=m_r.at[k],
            device_id=part_peer(k), device_id_type=MESH,
        )

    def sum_copy(k, slot):
        return pltpu.make_async_remote_copy(
            src_ref=nsend, dst_ref=nrecv.at[slot], send_sem=n_s.at[k], recv_sem=n_r.at[k],
            device_id=part_peer(k), device_id_type=MESH,
        )

    def each(count, do):
        def step(k, _):
            do(k)
            return 0

        lax.fori_loop(1, count, step, 0)

    def compute(p):
        quarter = p // PIECES
        h = lax.rem(p, PIECES)

        def chunk(c, _):
            inside = pl.multiple_of(h * width + c * TILE, TILE)
            base = pl.multiple_of(quarter * slab + inside, TILE)
            acc = jnp.zeros((TILE, LANES), F32)
            for k in range(TAPS):
                acc = acc + taps_ref[k : k + 1, :] * ext_ref[pl.ds(base + k, TILE), :]
            block = acc.T.astype(BF16)
            for b in range(BANDS):
                fsend[b * split + quarter, :, pl.ds(inside, TILE)] = block[b * det : (b + 1) * det, :]
            return 0

        lax.fori_loop(0, width // TILE, chunk, 0)

    def send_piece(p):
        quarter = p // PIECES
        h = lax.rem(p, PIECES)

        def send(k):
            if split == 1:
                signal_copy(h, k, me).start()
            else:

                @pl.when(lax.rem(td_peer(k), split) == quarter)
                def _():
                    signal_copy(h, k, me).start()

        each(td, send)

    compute(jnp.int32(0))
    pl.semaphore_wait(barrier, td - 1 + parts - 1)
    each(td, lambda k: tile_copy(k, me).start())
    send_piece(jnp.int32(0))

    def later(p, _):
        compute(p)
        send_piece(p)
        return 0

    lax.fori_loop(1, split * PIECES, later, 0)
    frecv[me] = fsend[me]

    rows = length * BANDS // TILE
    mask_ref[...] = scan_mask(bounds_ref, rows, n_bounds)
    weight_lanes = own_weights(weights_ref, me * det, det, dets)
    each(td, lambda k: tile_copy(k, td_source(k)).wait_recv())
    which = lax.broadcasted_iota(jnp.int32, (rows, LANES), 1).astype(F32)
    chosen_tile = jnp.where(trecv[...].reshape(rows, LANES) == which, 1.0, 0.0)
    by_block = chosen_tile[:, 0:TILES].astype(BF16)
    by_tile = chosen_tile.T[0:TILES, :].astype(BF16)
    counts = jnp.dot(by_tile, mask_ref[...].astype(BF16), preferred_element_type=F32)
    weight_rows = jnp.broadcast_to(weight_lanes, (LANES, LANES)).T[0:det, :]
    hits = jnp.concatenate([counts, weight_rows], axis=0).astype(BF16)
    msend[...] = hits
    mrecv[member] = hits
    each(parts, lambda k: hit_copy(k, member).start())
    p_high, p_low = projector(pos_ref, wafer_ref, dets)

    for h in range(PIECES):
        each(td, lambda k: signal_copy(h, k, td_source(k)).wait_recv())
        cols = slice(h * width, (h + 1) * width)
        cleaned = clean(p_high, p_low, frecv[:, :, cols].reshape(dets, width))
        csend[:, :, cols] = cleaned.reshape(td, det, width)
        each(td, lambda k: clean_copy(h, k, me).start())
    crecv[me] = csend[me]

    for h in range(PIECES):
        each(td, lambda k: clean_copy(h, k, td_source(k)).wait_recv())
        for n in range(rows):
            if (n % blocks) * TILE // width != h:
                continue
            inside = n % blocks
            cols = slice(inside * TILE, (inside + 1) * TILE)
            clean_ref[n * det : (n + 1) * det, :] = crecv[n // blocks, :, cols].astype(F32)
    for d in range(det):
        masked = (clean_ref[pl.ds(d, rows, stride=det), :] * mask_ref[...]).astype(BF16)
        sums = jnp.dot(by_tile, masked, preferred_element_type=F32) * weight_rows[d : d + 1, :]
        nsend[d * TILES : (d + 1) * TILES, :] = sums.astype(BF16)
    nrecv[member] = nsend[...]
    each(parts, lambda k: sum_copy(k, member).start())
    build_toeplitz(low_ref, last_ref, toep_ref, det)
    each(parts, lambda k: hit_copy(k, part_source(k)).wait_recv())
    hit = jnp.zeros((det, TILES, TILE), F32)
    for m in range(parts):
        part = mrecv[m].astype(F32)
        hit = hit + part[TILES:, None, :] * part[None, :TILES, :]
    each(parts, lambda k: sum_copy(k, part_source(k)).wait_recv())
    total = nrecv[0].astype(F32)
    for m in range(1, parts):
        total = total + nrecv[m].astype(F32)
    sky = total / (hit.reshape(det * TILES, TILE) + prior_weight)
    sky_ref[...] = sky
    def row_place(j):
        return pl.ds(pl.multiple_of(lax.rem(first_row + own_rows * j, det) * TILES, TILES), own_rows * TILES)

    def row_copy(j):
        return pltpu.make_async_remote_copy(
            src_ref=sky_ref.at[row_place(j)], dst_ref=skyrecv, send_sem=k_s.at[j], recv_sem=k_r,
            device_id=(obs, fold * per_fold + j), device_id_type=MESH,
        )

    def row_moves(do):
        for j in range(per_fold):
            holds = (first_row + own_rows * j) // det == lax.rem(me, per_fold)

            @pl.when(holds & (fold * per_fold + j != me))
            def _():
                do(j)

    row_moves(lambda j: row_copy(j).start())

    @pl.when(row_source == me)
    def _():
        skyrecv[...] = sky_ref[row_place(lax.rem(me, per_fold)), :]

    sky_b = sky.astype(BF16)
    zero = jnp.zeros((8, LANES), F32)
    near = lax.broadcasted_iota(jnp.int32, (rows, LANES), 1) < HALF
    per_band = rows // BANDS
    for d in range(det):
        picked = jnp.dot(by_block, sky_b[d * TILES : (d + 1) * TILES, :], preferred_element_type=F32)
        residual = mask_ref[...] * (clean_ref[pl.ds(d, rows, stride=det), :] - picked)
        spread = [
            jnp.dot(
                residual[b * per_band : (b + 1) * per_band, :].astype(BF16),
                toep_ref[d * BANDS + b],
                preferred_element_type=F32,
            )
            for b in range(BANDS)
        ]
        edge_ref[d, 0:8, :] = zero
        edge_ref[d, 8 + rows : 16 + rows, :] = zero
        edge_ref[d, 8 : 8 + rows, :] = jnp.concatenate([p[:, LANES:] for p in spread], axis=0)
        here = jnp.concatenate([p[:, :LANES] for p in spread], axis=0)
        away = jnp.where(near, edge_ref[d, 7 : 7 + rows, :], edge_ref[d, 9 : 9 + rows, :])
        wide_ref[pl.ds(d, rows, stride=det), :] = here + away
    for n in range(rows):
        out_ref[:, n * TILE : (n + 1) * TILE] = wide_ref[n * det : (n + 1) * det, :]

    @pl.when(row_source != me)
    def _():
        row_copy(0).wait_recv()

    row_moves(lambda j: row_copy(j).wait_send())
    for d in range(own_rows):
        skyout_ref[:, d, :] = skyrecv[d * TILES : (d + 1) * TILES, :]
    each(td, lambda k: tile_copy(k, me).wait_send())
    for h in range(PIECES):
        each(td, lambda k: signal_copy(h, k, me).wait_send())
        each(td, lambda k: clean_copy(h, k, me).wait_send())
    each(parts, lambda k: hit_copy(k, member).wait_send())
    each(parts, lambda k: sum_copy(k, member).wait_send())


VM = pl.BlockSpec(memory_space=pltpu.VMEM)
SM = pl.BlockSpec(memory_space=pltpu.SMEM)
HB = pl.BlockSpec(memory_space=pltpu.HBM)


def local(timestreams, filter_taps, scan_bounds, tile_index, det_weights, positions, wafer_group):
    _, det, samples = timestreams.shape
    td = lax.axis_size("td")
    n_obs = lax.axis_size("obs")
    dets = det * td
    length = samples // BANDS
    slab = samples // td
    blocks = slab // TILE
    parts = n_obs * (dets // TILE)
    own_rows = TILE // (n_obs * td)
    dims = (n_obs, td, det, length, slab, scan_bounds.shape[1])
    rows = samples // TILE
    dma = pltpu.SemaphoreType.DMA
    out, sky = pl.pallas_call(
        functools.partial(whole_kernel, dims),
        out_shape=(
            jax.ShapeDtypeStruct((det, samples), F32),
            jax.ShapeDtypeStruct((TILES, own_rows, TILE), F32),
        ),
        in_specs=[SM, SM, HB, HB, VM, VM, VM],
        out_specs=(VM, VM),
        scratch_shapes=[
            pltpu.VMEM((det, samples), BF16),
            pltpu.VMEM((det, BANDS, TAPS), BF16),
            pltpu.VMEM((det * BANDS, LANES), F32),
            pltpu.VMEM((det * BANDS, LANES), F32),
            pltpu.VMEM((TAPS, LANES), F32),
            pltpu.VMEM((det * BANDS, TILE, 2 * LANES), BF16),
            pltpu.VMEM((rows * det, TILE), F32),
            pltpu.VMEM((det, rows + 16, LANES), F32),
            pltpu.VMEM((rows * det, TILE), F32),
            pltpu.VMEM((length + 2 * HALF, LANES), F32),
            pltpu.VMEM((rows, TILE), F32),
            pltpu.VMEM((td, det, slab), BF16),
            pltpu.VMEM((td, det, slab), BF16),
            pltpu.VMEM((td, det, slab), BF16),
            pltpu.VMEM((td, det, slab), BF16),
            pltpu.VMEM((blocks, LANES), F32),
            pltpu.VMEM((td, blocks, LANES), F32),
            pltpu.VMEM((TILES + det, TILE), BF16),
            pltpu.VMEM((parts, TILES + det, TILE), BF16),
            pltpu.VMEM((det * TILES, TILE), BF16),
            pltpu.VMEM((parts, det * TILES, TILE), BF16),
            pltpu.VMEM((det * TILES, TILE), F32),
            pltpu.VMEM((own_rows * TILES, TILE), F32),
            dma((PIECES, td)), dma((PIECES, td)), dma((PIECES, td)), dma((PIECES, td)),
            dma((td,)), dma((td,)), dma((parts,)), dma((parts,)),
            dma((parts,)), dma((parts,)),
            dma((td // (dets // TILE),)), dma, dma((2,)),
        ],
        compiler_params=pltpu.CompilerParams(
            collective_id=0, has_side_effects=True, vmem_limit_bytes=48 << 20
        ),
    )(
        scan_bounds, tile_index, timestreams[0], filter_taps[0], det_weights, positions,
        wafer_group.reshape(1, dets),
    )
    return out[None], sky


def solution(mesh):
    placed = (
        P("obs", "td", None),
        P("obs", "td", None, None),
        P("obs", None),
        P("obs", "td"),
        P("obs", None),
        P(),
        P(),
    )
    return jax.shard_map(
        local,
        mesh=mesh,
        in_specs=placed,
        out_specs=(P("obs", "td", None), P(None, ("obs", "td"), None)),
        check_vma=False,
    )
```
